768 devices in a mesh: lat: 128 (over x, z_hi, y), ma: 6 (over z_lo, core).
Axes of the slice: x: 4, y: 8, z: 12 (z_hi: 4, z_lo: 3; z = z_hi * 3 + z_lo), core: 2. Of those that a mesh axis runs over, the one named last changes fastest.
Arguments:
- grad_fourier: bfloat16 [12, 8192, 2, 384], P('ma', 'lat'), may hold values from -6 to 6
- legendre: bfloat16 [12, 8192, 640], P('ma', 'lat'), may hold values from -0.0625 to 0.0625
- spectra: bfloat16 [640, 12, 2, 384], P('lat', None, None, 'ma'), may hold values from -1.75 to 1.75
- filter_weight: float32 [640, 2, 384], P('lat'), may hold values from -6 to 6
Outputs:
- input_grad: float32 [640, 12, 2, 384], P('lat', 'ma')
- weight_grad: float32 [640, 2, 384], P('lat', None, 'ma')
The draws below stay inside these ranges and needn't reach their ends.
All inputs are finite; a program needn't handle non-finite values.
Results may differ from the reference program's by a relative error of at most 0.0006.
Values may be sent and summed in bfloat16 or wider, within the bound.
No kernel may reach another device: no remote copies, remote signals or barrier semaphores. Data moves between devices by JAX's collectives and lax.ppermute only.
A program may use at most 32 MiB of HBM per device.

```python
import jax
import jax.numpy as jnp
from jax import lax

C = 384
L = 640
NLAT = 8192
M = 12


def levels(stream_key, extent, shards, smallest, largest):
    def one(dim, blocks):
        draws = jax.random.uniform(jax.random.fold_in(jax.random.fold_in(stream_key, 6), dim), (blocks,), jnp.float32, smallest / len(shards), largest / len(shards))
        return jnp.repeat(jnp.exp(draws), extent[dim] // blocks).reshape((-1,) + (1,) * (len(extent) - dim - 1))

    loudness = one(*shards[0])
    for cut in shards[1:]:
        loudness = loudness * one(*cut)
    return loudness


def bell_draw(rng, extent, spread, bound, split=(), held_as=jnp.bfloat16):
    entries = spread * jax.random.normal(rng, extent, jnp.float32)
    if split:
        entries = entries * levels(rng, extent, split, -0.22, 0.18)
    return jnp.clip(entries, -bound, bound).astype(held_as)


def setup_inputs(seed: int = 0) -> dict:
    splits = jax.random.split(jax.random.key(seed), 5)
    grad_fourier = bell_draw(splits[0], (M, NLAT, 2, C), 1.0, 6.0, ((0, 6), (1, 128)))
    legendre = bell_draw(splits[1], (M, NLAT, L), NLAT ** -0.5, 0.0625, ((0, 6), (1, 128)))
    spectra = bell_draw(splits[2], (L, M, 2, C), M ** -0.5, 1.75, ((0, 128), (3, 6)))
    filter_weight = bell_draw(splits[3], (L, 2, C), 1.0, 6.0, ((0, 128),), jnp.float32)
    return {"grad_fourier": grad_fourier, "legendre": legendre, "spectra": spectra, "filter_weight": filter_weight}


def reference(grad_fourier, legendre, spectra, filter_weight):
    degrees = jnp.arange(L, dtype=jnp.int32)

    def analyse(order):
        column = lax.dynamic_index_in_dim(legendre, order, 0, keepdims=False)
        table = jnp.where(degrees[None, :] >= order, column, jnp.zeros_like(column))
        rows = lax.dynamic_index_in_dim(grad_fourier, order, 0, keepdims=False)
        flat = rows.reshape(NLAT, 2 * C)
        return jnp.dot(table.T, flat, preferred_element_type=jnp.float32).reshape(L, 2, C)

    stacked = lax.map(analyse, jnp.arange(M, dtype=jnp.int32))
    grads = jnp.transpose(stacked, (1, 0, 2, 3))
    real_grad = grads[:, :, 0, :]
    imag_grad = grads[:, :, 1, :]
    real_weight = filter_weight[:, None, 0, :]
    imag_weight = filter_weight[:, None, 1, :]
    input_grad = jnp.stack([real_weight * real_grad + imag_weight * imag_grad,
                            real_weight * imag_grad - imag_weight * real_grad], axis=2)
    stored = spectra.astype(jnp.float32)
    real_store = stored[:, :, 0, :]
    imag_store = stored[:, :, 1, :]
    weight_grad = jnp.stack([jnp.sum(real_store * real_grad + imag_store * imag_grad, axis=1),
                             jnp.sum(real_store * imag_grad - imag_store * real_grad, axis=1)], axis=1)
    return input_grad, weight_grad
```

```python
import jax
import jax.numpy as jnp
from jax import lax
from jax.experimental import pallas as pl
from jax.experimental.pallas import tpu as pltpu
from jax.sharding import Mesh, PartitionSpec as P

BF, F16, F32 = jnp.bfloat16, jnp.float16, jnp.float32
AXES = ("x", "zh", "yh", "yl", "zl", "core")
LEVELS = 7


def pack_kernel(order_ref, grad_ref, leg_ref, out_ref):
    eye = jnp.where(
        lax.broadcasted_iota(jnp.int32, (128, 128), 0) == lax.broadcasted_iota(jnp.int32, (128, 128), 1), 1.0, 0.0
    ).astype(BF)
    order = order_ref[0] + jnp.where(lax.broadcasted_iota(jnp.int32, (128, 128), 1) >= 64, 1, 0)
    ahead = lax.broadcasted_iota(jnp.int32, (128, 128), 0) - order
    tiles = []
    for k in range(5):
        turned = lax.dot_general(
            eye, leg_ref[:, 128 * k:128 * (k + 1)], (((1,), (1,)), ((), ())), preferred_element_type=F32
        )
        tiles.append(jnp.where(ahead >= -128 * k, turned, 0.0).astype(BF))
    table = jnp.concatenate(tiles, axis=0)
    grad = [grad_ref[:, :, r, :].reshape(128, 384) for r in range(2)]
    for x in range(4):
        for r in range(2):
            out_ref[2 * x + r, 0:160, :] = table[x * 160:(x + 1) * 160]
            for j in range(3):
                out_ref[2 * x + r, 160 + 128 * j:288 + 128 * j, :] = grad[r][:, 128 * j:128 * (j + 1)]


def mm_kernel(in_ref, out_ref, acc_ref):
    n = lax.broadcasted_iota(jnp.int32, (160, 160), 0)
    src = (n % 4) * 40 + ((n % 32) // 4) * 5 + n // 32
    pick = jnp.where(lax.broadcasted_iota(jnp.int32, (160, 160), 1) == src, 1.0, 0.0).astype(BF)
    table = jnp.concatenate([in_ref[s, 0:160, :] for s in range(8)], axis=1)
    table = jnp.dot(pick, table, preferred_element_type=F32)
    early = lax.broadcasted_iota(jnp.int32, (160, 128), 1) < 64
    accs = []
    for m in range(2):
        lhs, rhs = [], []
        for s in range(0, 8, 2):
            one, two = table[:, 128 * s:128 * (s + 1)], table[:, 128 * (s + 1):128 * (s + 2)]
            if m == 0:
                pair = jnp.where(early, one, pltpu.roll(two, 64, 1))
            else:
                pair = jnp.where(early, pltpu.roll(one, 64, 1), two)
            lhs.append(pair.astype(BF))
            for t in (s, s + 1):
                rhs.append(
                    jnp.concatenate(
                        [in_ref[t, 160 + 128 * j + 64 * m:224 + 128 * j + 64 * m, :] for j in range(3)], axis=1
                    )
                )
        accs.append(
            jnp.dot(jnp.concatenate(lhs, axis=1), jnp.concatenate(rhs, axis=0), preferred_element_type=F32)
        )
    top = jnp.maximum(jnp.max(jnp.abs(accs[0])), jnp.max(jnp.abs(accs[1])))
    up, code = jnp.float32(2.0**8), jnp.float32(0.0)
    for k in range(1, LEVELS):
        small = top < 2.0 ** (7 - 18 * k)
        up = jnp.where(small, jnp.float32(2.0 ** (8 + 18 * k)), up)
        code = jnp.where(small, jnp.float32(k), code)
    for j in range(3):
        for m in range(2):
            part = (accs[m][:, 128 * j:128 * (j + 1)] * up).reshape(5, 4, 8, 128)
            for i in range(5):
                for d in range(4):
                    acc_ref[d, i * 6 + m * 3 + j] = part[i, d]
    for d in range(4):
        acc_ref[d, 30:32] = jnp.full((2, 8, 128), code, F32)
        out_ref[8 * d:8 * (d + 1)] = jnp.swapaxes(acc_ref[d], 0, 1)


def body(grad_fourier, legendre, spectra, filter_weight):
    first = ((lax.axis_index("zl") * 2 + lax.axis_index("core")) * 2).astype(jnp.int32).reshape(1)
    vm = pl.BlockSpec(memory_space=pltpu.VMEM)
    send = pl.pallas_call(
        pack_kernel,
        out_shape=jax.ShapeDtypeStruct((8, 544, 128), BF),
        in_specs=[pl.BlockSpec(memory_space=pltpu.SMEM), vm, vm],
        out_specs=vm,
    )(first, grad_fourier, legendre.reshape(128, 640))
    got = lax.all_to_all(send, ("x", "yl"), 0, 0)
    part = pl.pallas_call(
        mm_kernel,
        out_shape=pltpu.VMEM((32, 32, 128), F32),
        in_specs=[vm],
        out_specs=vm,
        scratch_shapes=[pltpu.VMEM((4, 32, 8, 128), F32)],
    )(got)
    part = lax.all_to_all(part.astype(F16), ("yh", "yl", "zh"), 0, 0)
    part = part.reshape(4, 2, 4, 32, 128).astype(F32)
    code, down = part[:, :, :, 30:31, :], jnp.float32(2.0**-8)
    for k in range(1, LEVELS):
        down = jnp.where(code == k, jnp.float32(2.0 ** -(8 + 18 * k)), down)
    part = jnp.sum(part * down, axis=(0, 2))
    grads = part[:, :30].reshape(2, 5, 2, 384)
    gre, gim = grads[0], grads[1]
    wre, wim = filter_weight[:, None, 0, :], filter_weight[:, None, 1, :]
    input_grad = jnp.stack([wre * gre + wim * gim, wre * gim - wim * gre], axis=2)
    blocks = grads.reshape(2, 5, 2, 6, 64).transpose(3, 1, 2, 0, 4).reshape(6, 10, 128)
    mine = lax.all_to_all(blocks, ("zl", "core"), 0, 0)
    mine = mine.reshape(6, 5, 2, 2, 64).transpose(1, 0, 2, 3, 4).reshape(5, 12, 2, 64)
    st = spectra.astype(F32)
    sre, sim = st[:, :, 0, :], st[:, :, 1, :]
    mre, mim = mine[:, :, 0, :], mine[:, :, 1, :]
    weight_grad = jnp.stack(
        [jnp.sum(sre * mre + sim * mim, axis=1), jnp.sum(sre * mim - sim * mre, axis=1)], axis=1
    )
    return input_grad, weight_grad


def solution(mesh):
    fine = Mesh(mesh.devices.reshape(4, 4, 4, 2, 3, 2), AXES)
    lat, ma = ("x", "zh", "yh", "yl"), ("zl", "core")
    in_specs = (P(ma, lat, None, None), P(ma, lat, None), P(lat, None, None, ma), P(lat, None, None))
    out_specs = (P(lat, ma, None, None), P(lat, None, ma))
    return jax.shard_map(body, mesh=fine, in_specs=in_specs, out_specs=out_specs, check_vma=False)
```

```python
import jax
import jax.numpy as jnp
from jax import lax
from jax.experimental import pallas as pl
from jax.experimental.pallas import tpu as pltpu
from jax.sharding import Mesh, PartitionSpec as P

BF, F16, F32 = jnp.bfloat16, jnp.float16, jnp.float32
AXES = ("x", "zh", "yh", "yl", "zl", "core")
LEVELS = 7


def pack_kernel(order_ref, grad_ref, leg_ref, out_ref):
    eye = jnp.where(
        lax.broadcasted_iota(jnp.int32, (128, 128), 0) == lax.broadcasted_iota(jnp.int32, (128, 128), 1), 1.0, 0.0
    ).astype(BF)
    order = order_ref[0] + jnp.where(lax.broadcasted_iota(jnp.int32, (128, 128), 1) >= 64, 1, 0)
    ahead = lax.broadcasted_iota(jnp.int32, (128, 128), 0) - order
    tiles = []
    for k in range(5):
        turned = lax.dot_general(
            eye, leg_ref[:, 128 * k:128 * (k + 1)], (((1,), (1,)), ((), ())), preferred_element_type=F32
        )
        tiles.append(jnp.where(ahead >= -128 * k, turned, 0.0).astype(BF))
    table = jnp.concatenate(tiles, axis=0)
    grad = [grad_ref[:, :, r, :].reshape(128, 384) for r in range(2)]
    for x in range(4):
        for r in range(2):
            out_ref[2 * x + r, 0:160, :] = table[x * 160:(x + 1) * 160]
            for j in range(3):
                out_ref[2 * x + r, 160 + 128 * j:288 + 128 * j, :] = grad[r][:, 128 * j:128 * (j + 1)]


def mm_kernel(in_ref, out_ref, acc_ref):
    n = lax.broadcasted_iota(jnp.int32, (160, 160), 0)
    src = (n % 4) * 40 + ((n % 32) // 4) * 5 + n // 32
    pick = jnp.where(lax.broadcasted_iota(jnp.int32, (160, 160), 1) == src, 1.0, 0.0).astype(BF)
    table = jnp.concatenate([in_ref[s, 0:160, :] for s in range(8)], axis=1)
    table = jnp.dot(pick, table, preferred_element_type=F32)
    early = lax.broadcasted_iota(jnp.int32, (160, 128), 1) < 64
    accs = []
    for m in range(2):
        lhs, rhs = [], []
        for s in range(0, 8, 2):
            one, two = table[:, 128 * s:128 * (s + 1)], table[:, 128 * (s + 1):128 * (s + 2)]
            if m == 0:
                pair = jnp.where(early, one, pltpu.roll(two, 64, 1))
            else:
                pair = jnp.where(early, pltpu.roll(one, 64, 1), two)
            lhs.append(pair.astype(BF))
            for t in (s, s + 1):
                rhs.append(
                    jnp.concatenate(
                        [in_ref[t, 160 + 128 * j + 64 * m:224 + 128 * j + 64 * m, :] for j in range(3)], axis=1
                    )
                )
        accs.append(
            jnp.dot(jnp.concatenate(lhs, axis=1), jnp.concatenate(rhs, axis=0), preferred_element_type=F32)
        )
    top = jnp.maximum(jnp.max(jnp.abs(accs[0])), jnp.max(jnp.abs(accs[1])))
    up, code = jnp.float32(2.0**8), jnp.float32(0.0)
    for k in range(1, LEVELS):
        small = top < 2.0 ** (7 - 18 * k)
        up = jnp.where(small, jnp.float32(2.0 ** (8 + 18 * k)), up)
        code = jnp.where(small, jnp.float32(k), code)
    for j in range(3):
        for m in range(2):
            part = (accs[m][:, 128 * j:128 * (j + 1)] * up).reshape(5, 4, 8, 128)
            for i in range(5):
                for d in range(4):
                    acc_ref[d, i * 6 + m * 3 + j] = part[i, d]
    for d in range(4):
        acc_ref[d, 30:32] = jnp.full((2, 8, 128), code, F32)
        out_ref[8 * d:8 * (d + 1)] = jnp.swapaxes(acc_ref[d], 0, 1)


def blocks_kernel(in_ref, out_ref):
    early = lax.broadcasted_iota(jnp.int32, (10, 128), 1) < 64
    for j in range(3):
        re, im = in_ref[0, pl.ds(j, 10, stride=3), :], in_ref[1, pl.ds(j, 10, stride=3), :]
        out_ref[2 * j] = jnp.where(early, re, pltpu.roll(im, 64, 1))
        out_ref[2 * j + 1] = jnp.where(early, pltpu.roll(re, 64, 1), im)


def weight_kernel(grad_ref, spec_ref, out_ref, sum_ref):
    total = jnp.zeros((10, 128), F32)
    early = lax.broadcasted_iota(jnp.int32, (10, 128), 1) < 64
    for k in range(6):
        grad, spec = grad_ref[k], spec_ref[k]
        same, cross = spec * grad, spec * pltpu.roll(grad, 64, 1)
        total = total + jnp.where(
            early, same + pltpu.roll(same, 64, 1), pltpu.roll(cross, 64, 1) - cross
        )
    sum_ref[0:10] = total
    both = sum_ref[pl.ds(0, 5, stride=2), :] + sum_ref[pl.ds(1, 5, stride=2), :]
    out_ref[:, 0, :] = both[:, 0:64]
    out_ref[:, 1, :] = both[:, 64:128]


def input_kernel(in_ref, weight_ref, spec_ref, out_ref, turned_ref):
    for j in range(3):
        wre, wim = (weight_ref[:, r, 128 * j:128 * (j + 1)] for r in range(2))
        for m in range(2):
            gre, gim = (in_ref[r, pl.ds(3 * m + j, 5, stride=6), :] for r in range(2))
            out_ref[:, m, 0, 128 * j:128 * (j + 1)] = wre * gre + wim * gim
            out_ref[:, m, 1, 128 * j:128 * (j + 1)] = wre * gim - wim * gre
    spec = jnp.concatenate([spec_ref[:, :, r, :].astype(F32) for r in range(2)], axis=2)
    for m in range(12):
        turned_ref[m // 2, pl.ds(m % 2, 5, stride=2), :] = spec[:, m, :]


def body(grad_fourier, legendre, spectra, filter_weight):
    first = ((lax.axis_index("zl") * 2 + lax.axis_index("core")) * 2).astype(jnp.int32).reshape(1)
    vm = pl.BlockSpec(memory_space=pltpu.VMEM)
    send = pl.pallas_call(
        pack_kernel,
        out_shape=pltpu.VMEM((8, 544, 128), BF),
        in_specs=[pl.BlockSpec(memory_space=pltpu.SMEM), vm, vm],
        out_specs=vm,
    )(first, grad_fourier, legendre.reshape(128, 640))
    got = pltpu.with_memory_space_constraint(lax.all_to_all(send, ("x", "yl"), 0, 0), pltpu.VMEM)
    part = pl.pallas_call(
        mm_kernel,
        out_shape=pltpu.VMEM((32, 32, 128), F32),
        in_specs=[vm],
        out_specs=vm,
        scratch_shapes=[pltpu.VMEM((4, 32, 8, 128), F32)],
    )(got)
    part = lax.all_to_all(part.astype(F16), ("yh", "yl", "zh"), 0, 0)
    part = part.reshape(4, 2, 4, 32, 128).astype(F32)
    code, down = part[:, :, :, 30:31, :], jnp.float32(2.0**-8)
    for k in range(1, LEVELS):
        down = jnp.where(code == k, jnp.float32(2.0 ** -(8 + 18 * k)), down)
    part = pltpu.with_memory_space_constraint(jnp.sum(part * down, axis=(0, 2)), pltpu.VMEM)
    blocks = pl.pallas_call(
        blocks_kernel, out_shape=jax.ShapeDtypeStruct((6, 10, 128), F32), in_specs=[vm], out_specs=vm
    )(part)
    mine = lax.all_to_all(blocks, ("zl", "core"), 0, 0)
    input_grad, spec = pl.pallas_call(
        input_kernel,
        out_shape=(jax.ShapeDtypeStruct((5, 2, 2, 384), F32), pltpu.VMEM((6, 10, 128), F32)),
        in_specs=[vm, vm, vm],
        out_specs=(vm, vm),
        cost_estimate=pl.CostEstimate(flops=100000, bytes_accessed=200000, transcendentals=0),
    )(part, filter_weight, spectra)
    weight_grad = pl.pallas_call(
        weight_kernel,
        out_shape=jax.ShapeDtypeStruct((5, 2, 64), F32),
        in_specs=[vm, vm],
        out_specs=vm,
        scratch_shapes=[pltpu.VMEM((16, 128), F32)],
    )(*(pltpu.with_memory_space_constraint(v, pltpu.VMEM) for v in (mine, spec)))
    return input_grad, weight_grad


def solution(mesh):
    fine = Mesh(mesh.devices.reshape(4, 4, 4, 2, 3, 2), AXES)
    lat, ma = ("x", "zh", "yh", "yl"), ("zl", "core")
    in_specs = (P(ma, lat, None, None), P(ma, lat, None), P(lat, None, None, ma), P(lat, None, None))
    out_specs = (P(lat, ma, None, None), P(lat, None, ma))
    return jax.shard_map(body, mesh=fine, in_specs=in_specs, out_specs=out_specs, check_vma=False)
```

```python
import jax
import jax.numpy as jnp
from jax import lax
from jax.experimental import pallas as pl
from jax.experimental.pallas import tpu as pltpu
from jax.sharding import Mesh, PartitionSpec as P

BF, F16, F32 = jnp.bfloat16, jnp.float16, jnp.float32
AXES = ("x", "zh", "yh", "yl", "zl", "core")
LEVELS = 7


def pack_kernel(order_ref, grad_ref, leg_ref, out_ref):
    eye = jnp.where(
        lax.broadcasted_iota(jnp.int32, (128, 128), 0) == lax.broadcasted_iota(jnp.int32, (128, 128), 1), 1.0, 0.0
    ).astype(BF)
    order = order_ref[0] + jnp.where(lax.broadcasted_iota(jnp.int32, (128, 128), 1) >= 64, 1, 0)
    ahead = lax.broadcasted_iota(jnp.int32, (128, 128), 0) - order
    tiles = []
    for k in range(5):
        turned = lax.dot_general(
            eye, leg_ref[:, 128 * k:128 * (k + 1)], (((1,), (1,)), ((), ())), preferred_element_type=F32
        )
        tiles.append(jnp.where(ahead >= -128 * k, turned, 0.0).astype(BF))
    table = jnp.concatenate(tiles, axis=0)
    grad = [grad_ref[:, :, r, :].reshape(128, 384) for r in range(2)]
    for x in range(4):
        for r in range(2):
            out_ref[2 * x + r, 0:160, :] = table[x * 160:(x + 1) * 160]
            for j in range(3):
                out_ref[2 * x + r, 160 + 128 * j:288 + 128 * j, :] = grad[r][:, 128 * j:128 * (j + 1)]


def mm_kernel(in_ref, out_ref, acc_ref):
    n = lax.broadcasted_iota(jnp.int32, (160, 160), 0)
    src = (n % 4) * 40 + ((n % 32) // 4) * 5 + n // 32
    pick = jnp.where(lax.broadcasted_iota(jnp.int32, (160, 160), 1) == src, 1.0, 0.0).astype(BF)
    table = jnp.concatenate([in_ref[s, 0:160, :] for s in range(8)], axis=1)
    table = jnp.dot(pick, table, preferred_element_type=F32)
    early = lax.broadcasted_iota(jnp.int32, (160, 128), 1) < 64
    accs = []
    for m in range(2):
        lhs, rhs = [], []
        for s in range(0, 8, 2):
            one, two = table[:, 128 * s:128 * (s + 1)], table[:, 128 * (s + 1):128 * (s + 2)]
            if m == 0:
                pair = jnp.where(early, one, pltpu.roll(two, 64, 1))
            else:
                pair = jnp.where(early, pltpu.roll(one, 64, 1), two)
            lhs.append(pair.astype(BF))
            for t in (s, s + 1):
                rhs.append(
                    jnp.concatenate(
                        [in_ref[t, 160 + 128 * j + 64 * m:224 + 128 * j + 64 * m, :] for j in range(3)], axis=1
                    )
                )
        accs.append(
            jnp.dot(jnp.concatenate(lhs, axis=1), jnp.concatenate(rhs, axis=0), preferred_element_type=F32)
        )
    top = jnp.maximum(jnp.max(jnp.abs(accs[0])), jnp.max(jnp.abs(accs[1])))
    up, code = jnp.float32(2.0**8), jnp.float32(0.0)
    for k in range(1, LEVELS):
        small = top < 2.0 ** (7 - 18 * k)
        up = jnp.where(small, jnp.float32(2.0 ** (8 + 18 * k)), up)
        code = jnp.where(small, jnp.float32(k), code)
    for j in range(3):
        for m in range(2):
            part = (accs[m][:, 128 * j:128 * (j + 1)] * up).reshape(5, 4, 8, 128)
            for i in range(5):
                for d in range(4):
                    acc_ref[d, i * 6 + m * 3 + j] = part[i, d]
    for d in range(4):
        acc_ref[d, 30:32] = jnp.full((2, 8, 128), code, F32)
        out_ref[8 * d:8 * (d + 1)] = jnp.swapaxes(acc_ref[d], 0, 1)


def blocks_kernel(in_ref, out_ref):
    early = lax.broadcasted_iota(jnp.int32, (10, 128), 1) < 64
    for j in range(3):
        re, im = in_ref[0, pl.ds(j, 10, stride=3), :], in_ref[1, pl.ds(j, 10, stride=3), :]
        out_ref[2 * j] = jnp.where(early, re, pltpu.roll(im, 64, 1))
        out_ref[2 * j + 1] = jnp.where(early, pltpu.roll(re, 64, 1), im)


def weight_kernel(grad_ref, spec_ref, out_ref, sum_ref):
    total = jnp.zeros((10, 128), F32)
    early = lax.broadcasted_iota(jnp.int32, (10, 128), 1) < 64
    for k in range(6):
        grad, spec = grad_ref[k], spec_ref[k]
        same, cross = spec * grad, spec * pltpu.roll(grad, 64, 1)
        total = total + jnp.where(
            early, same + pltpu.roll(same, 64, 1), pltpu.roll(cross, 64, 1) - cross
        )
    sum_ref[0:10] = total
    both = sum_ref[pl.ds(0, 5, stride=2), :] + sum_ref[pl.ds(1, 5, stride=2), :]
    out_ref[:, 0, :] = both[:, 0:64]
    out_ref[:, 1, :] = both[:, 64:128]


def input_kernel(in_ref, weight_ref, spec_ref, out_ref, turned_ref):
    for j in range(3):
        wre, wim = (weight_ref[:, r, 128 * j:128 * (j + 1)] for r in range(2))
        for m in range(2):
            gre, gim = (in_ref[r, pl.ds(3 * m + j, 5, stride=6), :] for r in range(2))
            out_ref[:, m, 0, 128 * j:128 * (j + 1)] = wre * gre + wim * gim
            out_ref[:, m, 1, 128 * j:128 * (j + 1)] = wre * gim - wim * gre
    spec = jnp.concatenate([spec_ref[:, :, r, :].astype(F32) for r in range(2)], axis=2)
    for m in range(12):
        turned_ref[m // 2, pl.ds(m % 2, 5, stride=2), :] = spec[:, m, :]


def body(grad_fourier, legendre, spectra, filter_weight):
    first = ((lax.axis_index("zl") * 2 + lax.axis_index("core")) * 2).astype(jnp.int32).reshape(1)
    vm = pl.BlockSpec(memory_space=pltpu.VMEM)
    send = pl.pallas_call(
        pack_kernel,
        out_shape=pltpu.VMEM((8, 544, 128), BF),
        in_specs=[pl.BlockSpec(memory_space=pltpu.SMEM), vm, vm],
        out_specs=vm,
    )(first, grad_fourier, legendre.reshape(128, 640))
    got = pltpu.with_memory_space_constraint(lax.all_to_all(send, ("x", "yl"), 0, 0), pltpu.VMEM)
    part = pl.pallas_call(
        mm_kernel,
        out_shape=pltpu.VMEM((32, 32, 128), F32),
        in_specs=[vm],
        out_specs=vm,
        scratch_shapes=[pltpu.VMEM((4, 32, 8, 128), F32)],
    )(got)
    part = lax.all_to_all(part.astype(F16).reshape(8, 128, 128), ("yh", "yl"), 0, 0)
    part = part.reshape(4, 2, 4, 32, 128).astype(F32)
    code, down = part[:, :, :, 30:31, :], jnp.float32(2.0**-8)
    for k in range(1, LEVELS):
        down = jnp.where(code == k, jnp.float32(2.0 ** -(8 + 18 * k)), down)
    part = jnp.sum(part * down, axis=0).transpose(1, 0, 2, 3).reshape(4, 64, 128)
    part = lax.all_to_all(part, "zh", 0, 0)
    part = jnp.sum(part.reshape(4, 2, 32, 128), axis=0)
    part = pltpu.with_memory_space_constraint(part, pltpu.VMEM)
    blocks = pl.pallas_call(
        blocks_kernel, out_shape=jax.ShapeDtypeStruct((6, 10, 128), F32), in_specs=[vm], out_specs=vm
    )(part)
    mine = lax.all_to_all(blocks, ("zl", "core"), 0, 0)
    input_grad, spec = pl.pallas_call(
        input_kernel,
        out_shape=(jax.ShapeDtypeStruct((5, 2, 2, 384), F32), pltpu.VMEM((6, 10, 128), F32)),
        in_specs=[vm, vm, vm],
        out_specs=(vm, vm),
        cost_estimate=pl.CostEstimate(flops=100000, bytes_accessed=200000, transcendentals=0),
    )(part, filter_weight, spectra)
    weight_grad = pl.pallas_call(
        weight_kernel,
        out_shape=jax.ShapeDtypeStruct((5, 2, 64), F32),
        in_specs=[vm, vm],
        out_specs=vm,
        scratch_shapes=[pltpu.VMEM((16, 128), F32)],
    )(*(pltpu.with_memory_space_constraint(v, pltpu.VMEM) for v in (mine, spec)))
    return input_grad, weight_grad


def solution(mesh):
    fine = Mesh(mesh.devices.reshape(4, 4, 4, 2, 3, 2), AXES)
    lat, ma = ("x", "zh", "yh", "yl"), ("zl", "core")
    in_specs = (P(ma, lat, None, None), P(ma, lat, None), P(lat, None, None, ma), P(lat, None, None))
    out_specs = (P(lat, ma, None, None), P(lat, None, ma))
    return jax.shard_map(body, mesh=fine, in_specs=in_specs, out_specs=out_specs, check_vma=False)
```

```python
import jax
import jax.numpy as jnp
from jax import lax
from jax.experimental import pallas as pl
from jax.experimental.pallas import tpu as pltpu
from jax.sharding import Mesh, PartitionSpec as P

BF, F16, F32 = jnp.bfloat16, jnp.float16, jnp.float32
AXES = ("x", "zh", "yh", "yl", "zl", "core")
LEVELS = 7


def pack_kernel(order_ref, grad_ref, leg_ref, out_ref):
    eye = jnp.where(
        lax.broadcasted_iota(jnp.int32, (128, 128), 0) == lax.broadcasted_iota(jnp.int32, (128, 128), 1), 1.0, 0.0
    ).astype(BF)
    order = order_ref[0] + jnp.where(lax.broadcasted_iota(jnp.int32, (128, 128), 1) >= 64, 1, 0)
    ahead = lax.broadcasted_iota(jnp.int32, (128, 128), 0) - order
    tiles = []
    for k in range(5):
        turned = lax.dot_general(
            eye, leg_ref[:, 128 * k:128 * (k + 1)], (((1,), (1,)), ((), ())), preferred_element_type=F32
        )
        tiles.append(jnp.where(ahead >= -128 * k, turned, 0.0).astype(BF))
    table = jnp.concatenate(tiles, axis=0)
    n = lax.broadcasted_iota(jnp.int32, (256, 256), 0)
    part = jnp.where(
        lax.broadcasted_iota(jnp.int32, (256, 256), 1) == (n % 128) * 2 + n // 128, 1.0, 0.0
    ).astype(BF)
    grad = jnp.dot(part, grad_ref[...].reshape(256, 384), preferred_element_type=F32).astype(BF)
    grad = [grad[128 * r:128 * (r + 1)] for r in range(2)]
    for x in range(4):
        for r in range(2):
            out_ref[2 * x + r, 0:160, :] = table[x * 160:(x + 1) * 160]
            for j in range(3):
                out_ref[2 * x + r, 160 + 128 * j:288 + 128 * j, :] = grad[r][:, 128 * j:128 * (j + 1)]


def mm_kernel(in_ref, out_ref, acc_ref):
    n = lax.broadcasted_iota(jnp.int32, (160, 160), 0)
    src = (n % 4) * 40 + ((n % 32) // 4) * 5 + n // 32
    pick = jnp.where(lax.broadcasted_iota(jnp.int32, (160, 160), 1) == src, 1.0, 0.0).astype(BF)
    table = jnp.concatenate([in_ref[s, 0:160, :] for s in range(8)], axis=1)
    table = jnp.dot(pick, table, preferred_element_type=F32)
    early = lax.broadcasted_iota(jnp.int32, (160, 128), 1) < 64
    accs = []
    for m in range(2):
        lhs, rhs = [], []
        for s in range(0, 8, 2):
            one, two = table[:, 128 * s:128 * (s + 1)], table[:, 128 * (s + 1):128 * (s + 2)]
            if m == 0:
                pair = jnp.where(early, one, pltpu.roll(two, 64, 1))
            else:
                pair = jnp.where(early, pltpu.roll(one, 64, 1), two)
            lhs.append(pair.astype(BF))
            for t in (s, s + 1):
                rhs.append(
                    jnp.concatenate(
                        [in_ref[t, 160 + 128 * j + 64 * m:224 + 128 * j + 64 * m, :] for j in range(3)], axis=1
                    )
                )
        accs.append(
            jnp.dot(jnp.concatenate(lhs, axis=1), jnp.concatenate(rhs, axis=0), preferred_element_type=F32)
        )
    top = jnp.maximum(jnp.max(jnp.abs(accs[0])), jnp.max(jnp.abs(accs[1])))
    up, code = jnp.float32(2.0**8), jnp.float32(0.0)
    for k in range(1, LEVELS):
        small = top < 2.0 ** (7 - 18 * k)
        up = jnp.where(small, jnp.float32(2.0 ** (8 + 18 * k)), up)
        code = jnp.where(small, jnp.float32(k), code)
    for j in range(3):
        for m in range(2):
            part = (accs[m][:, 128 * j:128 * (j + 1)] * up).reshape(5, 4, 8, 128)
            for i in range(5):
                for d in range(4):
                    acc_ref[d, i * 6 + m * 3 + j] = part[i, d]
    for d in range(4):
        acc_ref[d, 30:32] = jnp.full((2, 8, 128), code, F32)
        out_ref[8 * d:8 * (d + 1)] = jnp.swapaxes(acc_ref[d], 0, 1)


def blocks_kernel(in_ref, out_ref):
    early = lax.broadcasted_iota(jnp.int32, (10, 128), 1) < 64
    for j in range(3):
        re, im = in_ref[0, pl.ds(j, 10, stride=3), :], in_ref[1, pl.ds(j, 10, stride=3), :]
        out_ref[2 * j] = jnp.where(early, re, pltpu.roll(im, 64, 1))
        out_ref[2 * j + 1] = jnp.where(early, pltpu.roll(re, 64, 1), im)


def weight_kernel(grad_ref, spec_ref, out_ref, sum_ref):
    total = jnp.zeros((10, 128), F32)
    early = lax.broadcasted_iota(jnp.int32, (10, 128), 1) < 64
    for k in range(6):
        grad, spec = grad_ref[k], spec_ref[k]
        same, cross = spec * grad, spec * pltpu.roll(grad, 64, 1)
        total = total + jnp.where(
            early, same + pltpu.roll(same, 64, 1), pltpu.roll(cross, 64, 1) - cross
        )
    sum_ref[0:10] = total
    both = sum_ref[pl.ds(0, 5, stride=2), :] + sum_ref[pl.ds(1, 5, stride=2), :]
    out_ref[:, 0, :] = both[:, 0:64]
    out_ref[:, 1, :] = both[:, 64:128]


def input_kernel(in_ref, weight_ref, spec_ref, out_ref, turned_ref):
    for j in range(3):
        wre, wim = (weight_ref[:, r, 128 * j:128 * (j + 1)] for r in range(2))
        for m in range(2):
            gre, gim = (in_ref[r, pl.ds(3 * m + j, 5, stride=6), :] for r in range(2))
            out_ref[:, m, 0, 128 * j:128 * (j + 1)] = wre * gre + wim * gim
            out_ref[:, m, 1, 128 * j:128 * (j + 1)] = wre * gim - wim * gre
    spec = jnp.concatenate([spec_ref[:, :, r, :].astype(F32) for r in range(2)], axis=2)
    for m in range(12):
        turned_ref[m // 2, pl.ds(m % 2, 5, stride=2), :] = spec[:, m, :]


def body(grad_fourier, legendre, spectra, filter_weight):
    first = ((lax.axis_index("zl") * 2 + lax.axis_index("core")) * 2).astype(jnp.int32).reshape(1)
    vm = pl.BlockSpec(memory_space=pltpu.VMEM)
    send = pl.pallas_call(
        pack_kernel,
        out_shape=pltpu.VMEM((8, 544, 128), BF),
        in_specs=[pl.BlockSpec(memory_space=pltpu.SMEM), vm, vm],
        out_specs=vm,
    )(first, grad_fourier, legendre.reshape(128, 640))
    got = pltpu.with_memory_space_constraint(lax.all_to_all(send, ("x", "yl"), 0, 0), pltpu.VMEM)
    part = pl.pallas_call(
        mm_kernel,
        out_shape=pltpu.VMEM((32, 32, 128), F32),
        in_specs=[vm],
        out_specs=vm,
        scratch_shapes=[pltpu.VMEM((4, 32, 8, 128), F32)],
    )(got)
    part = lax.all_to_all(part.astype(F16), ("yh", "yl", "zh"), 0, 0)
    part = part.reshape(4, 2, 4, 32, 128).astype(F32)
    code, down = part[:, :, :, 30:31, :], jnp.float32(2.0**-8)
    for k in range(1, LEVELS):
        down = jnp.where(code == k, jnp.float32(2.0 ** -(8 + 18 * k)), down)
    part = pltpu.with_memory_space_constraint(jnp.sum(part * down, axis=(0, 2)), pltpu.VMEM)
    blocks = pl.pallas_call(
        blocks_kernel, out_shape=jax.ShapeDtypeStruct((6, 10, 128), F32), in_specs=[vm], out_specs=vm
    )(part)
    mine = lax.all_to_all(blocks, ("zl", "core"), 0, 0)
    input_grad, spec = pl.pallas_call(
        input_kernel,
        out_shape=(jax.ShapeDtypeStruct((5, 2, 2, 384), F32), pltpu.VMEM((6, 10, 128), F32)),
        in_specs=[vm, vm, vm],
        out_specs=(vm, vm),
        cost_estimate=pl.CostEstimate(flops=100000, bytes_accessed=200000, transcendentals=0),
    )(part, filter_weight, spectra)
    weight_grad = pl.pallas_call(
        weight_kernel,
        out_shape=jax.ShapeDtypeStruct((5, 2, 64), F32),
        in_specs=[vm, vm],
        out_specs=vm,
        scratch_shapes=[pltpu.VMEM((16, 128), F32)],
    )(*(pltpu.with_memory_space_constraint(v, pltpu.VMEM) for v in (mine, spec)))
    return input_grad, weight_grad


def solution(mesh):
    fine = Mesh(mesh.devices.reshape(4, 4, 4, 2, 3, 2), AXES)
    lat, ma = ("x", "zh", "yh", "yl"), ("zl", "core")
    in_specs = (P(ma, lat, None, None), P(ma, lat, None), P(lat, None, None, ma), P(lat, None, None))
    out_specs = (P(lat, ma, None, None), P(lat, None, ma))
    return jax.shard_map(body, mesh=fine, in_specs=in_specs, out_specs=out_specs, check_vma=False)
```

```python
import jax
import jax.numpy as jnp
from jax import lax
from jax.experimental import pallas as pl
from jax.experimental.pallas import tpu as pltpu
from jax.sharding import Mesh, PartitionSpec as P

BF, F16, F32 = jnp.bfloat16, jnp.float16, jnp.float32
AXES = ("x", "zh", "yh", "yl", "zl", "core")
LEVELS = 7


def pack_kernel(order_ref, grad_ref, leg_ref, out_ref):
    eye = jnp.where(
        lax.broadcasted_iota(jnp.int32, (128, 128), 0) == lax.broadcasted_iota(jnp.int32, (128, 128), 1), 1.0, 0.0
    ).astype(BF)
    order = order_ref[0] + jnp.where(lax.broadcasted_iota(jnp.int32, (128, 128), 1) >= 64, 1, 0)
    ahead = lax.broadcasted_iota(jnp.int32, (128, 128), 0) - order
    tiles = []
    for k in range(5):
        turned = lax.dot_general(
            eye, leg_ref[:, 128 * k:128 * (k + 1)], (((1,), (1,)), ((), ())), preferred_element_type=F32
        )
        tiles.append(jnp.where(ahead >= -128 * k, turned, 0.0))
    table = jnp.concatenate(tiles, axis=0)
    n = lax.broadcasted_iota(jnp.int32, (256, 256), 0)
    part = jnp.where(
        lax.broadcasted_iota(jnp.int32, (256, 256), 1) == (n % 128) * 2 + n // 128, 1.0, 0.0
    ).astype(BF)
    grad = jnp.dot(part, grad_ref[...].reshape(256, 384), preferred_element_type=F32).astype(BF)
    early = lax.broadcasted_iota(jnp.int32, (80, 128), 1) < 64
    for x in range(4):
        one, two = table[160 * x:160 * x + 80], table[160 * x + 80:160 * x + 160]
        halves = (
            jnp.where(early, one, pltpu.roll(two, 64, 1)),
            jnp.where(early, pltpu.roll(one, 64, 1), two),
        )
        for m in range(2):
            out_ref[2 * x + m, 0:80, :] = halves[m].astype(BF)
            for r in range(2):
                for j in range(3):
                    row = 80 + 64 * (3 * r + j)
                    out_ref[2 * x + m, row:row + 64, :] = grad[
                        128 * r + 64 * m:128 * r + 64 * m + 64, 128 * j:128 * (j + 1)
                    ]


def mm_kernel(in_ref, out_ref, acc_ref):
    n = lax.broadcasted_iota(jnp.int32, (160, 160), 0)
    src = (n % 4) * 40 + ((n % 32) // 4) * 5 + n // 32
    pick = jnp.where(lax.broadcasted_iota(jnp.int32, (160, 160), 1) == src, 1.0, 0.0).astype(BF)
    early = lax.broadcasted_iota(jnp.int32, (80, 128), 1) < 64
    low, high, rhs = [], [], []
    for s in range(0, 8, 2):
        one, two = in_ref[s, 0:80, :].astype(F32), in_ref[s + 1, 0:80, :].astype(F32)
        low.append(jnp.where(early, one, pltpu.roll(two, 64, 1)).astype(BF))
        high.append(jnp.where(early, pltpu.roll(one, 64, 1), two).astype(BF))
    for s in range(8):
        rhs.append(jnp.concatenate([in_ref[s, 80 + 64 * j:144 + 64 * j, :] for j in range(6)], axis=1))
    table = jnp.concatenate([jnp.concatenate(low, axis=1), jnp.concatenate(high, axis=1)], axis=0)
    table = jnp.dot(pick, table, preferred_element_type=F32).astype(BF)
    acc = jnp.dot(table, jnp.concatenate(rhs, axis=0), preferred_element_type=F32)
    top = jnp.max(jnp.abs(acc))
    up, code = jnp.float32(2.0**8), jnp.float32(0.0)
    for k in range(1, LEVELS):
        small = top < 2.0 ** (7 - 18 * k)
        up = jnp.where(small, jnp.float32(2.0 ** (8 + 18 * k)), up)
        code = jnp.where(small, jnp.float32(k), code)
    for j in range(6):
        part = (acc[:, 128 * j:128 * (j + 1)] * up).reshape(5, 4, 8, 128)
        for i in range(5):
            for d in range(4):
                acc_ref[d, i * 6 + j] = part[i, d]
    for d in range(4):
        acc_ref[d, 30:32] = jnp.full((2, 8, 128), code, F32)
        out_ref[8 * d:8 * (d + 1)] = jnp.swapaxes(acc_ref[d], 0, 1)


def blocks_kernel(in_ref, out_ref):
    early = lax.broadcasted_iota(jnp.int32, (5, 128), 1) < 64
    for m in range(2):
        for j in range(3):
            re, im = (in_ref[m, pl.ds(3 * r + j, 5, stride=6), :] for r in range(2))
            out_ref[2 * j, 5 * m:5 * m + 5] = jnp.where(early, re, pltpu.roll(im, 64, 1))
            out_ref[2 * j + 1, 5 * m:5 * m + 5] = jnp.where(early, pltpu.roll(re, 64, 1), im)


def weight_kernel(grad_ref, spec_ref, out_ref, sum_ref):
    total = jnp.zeros((10, 128), F32)
    early = lax.broadcasted_iota(jnp.int32, (10, 128), 1) < 64
    for k in range(6):
        grad, spec = grad_ref[k], spec_ref[k]
        same, cross = spec * grad, spec * pltpu.roll(grad, 64, 1)
        total = total + jnp.where(
            early, same + pltpu.roll(same, 64, 1), pltpu.roll(cross, 64, 1) - cross
        )
    sum_ref[0:10] = total
    both = sum_ref[0:5] + sum_ref[5:10]
    out_ref[:, 0, :] = both[:, 0:64]
    out_ref[:, 1, :] = both[:, 64:128]


def input_kernel(in_ref, weight_ref, spec_ref, out_ref, turned_ref):
    for j in range(3):
        wre, wim = (weight_ref[:, r, 128 * j:128 * (j + 1)] for r in range(2))
        for m in range(2):
            gre, gim = (in_ref[m, pl.ds(3 * r + j, 5, stride=6), :] for r in range(2))
            out_ref[:, m, 0, 128 * j:128 * (j + 1)] = wre * gre + wim * gim
            out_ref[:, m, 1, 128 * j:128 * (j + 1)] = wre * gim - wim * gre
    spec = jnp.concatenate([spec_ref[:, :, r, :].astype(F32) for r in range(2)], axis=2)
    for m in range(12):
        turned_ref[m // 2, 5 * (m % 2):5 * (m % 2) + 5] = spec[:, m, :]


def body(grad_fourier, legendre, spectra, filter_weight):
    first = ((lax.axis_index("zl") * 2 + lax.axis_index("core")) * 2).astype(jnp.int32).reshape(1)
    vm = pl.BlockSpec(memory_space=pltpu.VMEM)
    send = pl.pallas_call(
        pack_kernel,
        out_shape=pltpu.VMEM((8, 464, 128), BF),
        in_specs=[pl.BlockSpec(memory_space=pltpu.SMEM), vm, vm],
        out_specs=vm,
    )(first, grad_fourier, legendre.reshape(128, 640))
    got = pltpu.with_memory_space_constraint(lax.all_to_all(send, ("x", "yl"), 0, 0), pltpu.VMEM)
    part = pl.pallas_call(
        mm_kernel,
        out_shape=pltpu.VMEM((32, 32, 128), F32),
        in_specs=[vm],
        out_specs=vm,
        scratch_shapes=[pltpu.VMEM((4, 32, 8, 128), F32)],
    )(got)
    part = lax.all_to_all(part.astype(F16), ("yh", "yl", "zh"), 0, 0)
    part = part.reshape(4, 2, 4, 32, 128).astype(F32)
    code, down = part[:, :, :, 30:31, :], jnp.float32(2.0**-8)
    for k in range(1, LEVELS):
        down = jnp.where(code == k, jnp.float32(2.0 ** -(8 + 18 * k)), down)
    part = pltpu.with_memory_space_constraint(jnp.sum(part * down, axis=(0, 2)), pltpu.VMEM)
    blocks = pl.pallas_call(
        blocks_kernel, out_shape=jax.ShapeDtypeStruct((6, 10, 128), F32), in_specs=[vm], out_specs=vm
    )(part)
    mine = lax.all_to_all(blocks, ("zl", "core"), 0, 0)
    input_grad, spec = pl.pallas_call(
        input_kernel,
        out_shape=(jax.ShapeDtypeStruct((5, 2, 2, 384), F32), pltpu.VMEM((6, 10, 128), F32)),
        in_specs=[vm, vm, vm],
        out_specs=(vm, vm),
        cost_estimate=pl.CostEstimate(flops=100000, bytes_accessed=200000, transcendentals=0),
    )(part, filter_weight, spectra)
    weight_grad = pl.pallas_call(
        weight_kernel,
        out_shape=jax.ShapeDtypeStruct((5, 2, 64), F32),
        in_specs=[vm, vm],
        out_specs=vm,
        scratch_shapes=[pltpu.VMEM((16, 128), F32)],
    )(*(pltpu.with_memory_space_constraint(v, pltpu.VMEM) for v in (mine, spec)))
    return input_grad, weight_grad


def solution(mesh):
    fine = Mesh(mesh.devices.reshape(4, 4, 4, 2, 3, 2), AXES)
    lat, ma = ("x", "zh", "yh", "yl"), ("zl", "core")
    in_specs = (P(ma, lat, None, None), P(ma, lat, None), P(lat, None, None, ma), P(lat, None, None))
    out_specs = (P(lat, ma, None, None), P(lat, None, ma))
    return jax.shard_map(body, mesh=fine, in_specs=in_specs, out_specs=out_specs, check_vma=False)
```

```python
import jax
import jax.numpy as jnp
from jax import lax
from jax.experimental import pallas as pl
from jax.experimental.pallas import tpu as pltpu
from jax.sharding import Mesh, PartitionSpec as P

BF, F16, F32 = jnp.bfloat16, jnp.float16, jnp.float32
AXES = ("x", "zh", "yh", "yl", "zl", "core")
LEVELS = 7


def pack_kernel(order_ref, grad_ref, leg_ref, out_ref):
    eye = jnp.where(
        lax.broadcasted_iota(jnp.int32, (128, 128), 0) == lax.broadcasted_iota(jnp.int32, (128, 128), 1), 1.0, 0.0
    ).astype(BF)
    order = order_ref[0] + jnp.where(lax.broadcasted_iota(jnp.int32, (128, 128), 1) >= 64, 1, 0)
    ahead = lax.broadcasted_iota(jnp.int32, (128, 128), 0) - order
    tiles = []
    for k in range(5):
        turned = lax.dot_general(
            eye, leg_ref[:, 128 * k:128 * (k + 1)], (((1,), (1,)), ((), ())), preferred_element_type=F32
        )
        tiles.append(jnp.where(ahead >= -128 * k, turned, 0.0))
    table = jnp.concatenate(tiles, axis=0)
    n = lax.broadcasted_iota(jnp.int32, (256, 256), 0)
    part = jnp.where(
        lax.broadcasted_iota(jnp.int32, (256, 256), 1) == (n % 128) * 2 + n // 128, 1.0, 0.0
    ).astype(BF)
    grad = jnp.dot(part, grad_ref[...].reshape(256, 384), preferred_element_type=F32).astype(BF)
    early = lax.broadcasted_iota(jnp.int32, (80, 128), 1) < 64
    for x in range(4):
        one, two = table[160 * x:160 * x + 80], table[160 * x + 80:160 * x + 160]
        halves = (
            jnp.where(early, one, pltpu.roll(two, 64, 1)),
            jnp.where(early, pltpu.roll(one, 64, 1), two),
        )
        for m in range(2):
            out_ref[4 * m + x, 0:80, :] = halves[m].astype(BF)
            for r in range(2):
                for j in range(3):
                    row = 80 + 64 * (3 * r + j)
                    out_ref[4 * m + x, row:row + 64, :] = grad[
                        128 * r + 64 * m:128 * r + 64 * m + 64, 128 * j:128 * (j + 1)
                    ]


def mm_kernel(in_ref, out_ref, acc_ref):
    n = lax.broadcasted_iota(jnp.int32, (160, 160), 0)
    src = (n % 4) * 40 + ((n % 32) // 4) * 5 + n // 32
    pick = jnp.where(lax.broadcasted_iota(jnp.int32, (160, 160), 1) == src, 1.0, 0.0).astype(BF)
    early = lax.broadcasted_iota(jnp.int32, (80, 128), 1) < 64
    low, high, rhs = [], [], []
    for s in range(0, 8, 2):
        one, two = in_ref[s, 0:80, :].astype(F32), in_ref[s + 1, 0:80, :].astype(F32)
        low.append(jnp.where(early, one, pltpu.roll(two, 64, 1)).astype(BF))
        high.append(jnp.where(early, pltpu.roll(one, 64, 1), two).astype(BF))
    for s in range(8):
        rhs.append(jnp.concatenate([in_ref[s, 80 + 64 * j:144 + 64 * j, :] for j in range(6)], axis=1))
    table = jnp.concatenate([jnp.concatenate(low, axis=1), jnp.concatenate(high, axis=1)], axis=0)
    table = jnp.dot(pick, table, preferred_element_type=F32).astype(BF)
    acc = jnp.dot(table, jnp.concatenate(rhs, axis=0), preferred_element_type=F32)
    top = jnp.max(jnp.abs(acc))
    up, code = jnp.float32(2.0**8), jnp.float32(0.0)
    for k in range(1, LEVELS):
        small = top < 2.0 ** (7 - 18 * k)
        up = jnp.where(small, jnp.float32(2.0 ** (8 + 18 * k)), up)
        code = jnp.where(small, jnp.float32(k), code)
    for j in range(6):
        part = (acc[:, 128 * j:128 * (j + 1)] * up).reshape(5, 4, 8, 128)
        for i in range(5):
            for d in range(4):
                acc_ref[d, i * 6 + j] = part[i, d]
    for d in range(4):
        acc_ref[d, 30:32] = jnp.full((2, 8, 128), code, F32)
        out_ref[8 * d:8 * (d + 1)] = jnp.swapaxes(acc_ref[d], 0, 1)


def blocks_kernel(in_ref, out_ref):
    early = lax.broadcasted_iota(jnp.int32, (5, 128), 1) < 64
    for m in range(2):
        for j in range(3):
            re, im = (in_ref[m, pl.ds(3 * r + j, 5, stride=6), :] for r in range(2))
            out_ref[2 * j, 5 * m:5 * m + 5] = jnp.where(early, re, pltpu.roll(im, 64, 1))
            out_ref[2 * j + 1, 5 * m:5 * m + 5] = jnp.where(early, pltpu.roll(re, 64, 1), im)


def weight_kernel(grad_ref, spec_ref, out_ref, sum_ref):
    total = jnp.zeros((10, 128), F32)
    early = lax.broadcasted_iota(jnp.int32, (10, 128), 1) < 64
    for k in range(6):
        grad, spec = grad_ref[k], spec_ref[k]
        same, cross = spec * grad, spec * pltpu.roll(grad, 64, 1)
        total = total + jnp.where(
            early, same + pltpu.roll(same, 64, 1), pltpu.roll(cross, 64, 1) - cross
        )
    sum_ref[0:10] = total
    both = sum_ref[0:5] + sum_ref[5:10]
    out_ref[:, 0, :] = both[:, 0:64]
    out_ref[:, 1, :] = both[:, 64:128]


def input_kernel(in_ref, weight_ref, spec_ref, out_ref, turned_ref):
    for j in range(3):
        wre, wim = (weight_ref[:, r, 128 * j:128 * (j + 1)] for r in range(2))
        for m in range(2):
            gre, gim = (in_ref[m, pl.ds(3 * r + j, 5, stride=6), :] for r in range(2))
            out_ref[:, m, 0, 128 * j:128 * (j + 1)] = wre * gre + wim * gim
            out_ref[:, m, 1, 128 * j:128 * (j + 1)] = wre * gim - wim * gre
    spec = jnp.concatenate([spec_ref[:, :, r, :].astype(F32) for r in range(2)], axis=2)
    for m in range(12):
        turned_ref[m // 2, 5 * (m % 2):5 * (m % 2) + 5] = spec[:, m, :]


def body(grad_fourier, legendre, spectra, filter_weight):
    first = ((lax.axis_index("zl") * 2 + lax.axis_index("core")) * 2).astype(jnp.int32).reshape(1)
    vm = pl.BlockSpec(memory_space=pltpu.VMEM)
    send = pl.pallas_call(
        pack_kernel,
        out_shape=pltpu.VMEM((8, 464, 128), BF),
        in_specs=[pl.BlockSpec(memory_space=pltpu.SMEM), vm, vm],
        out_specs=vm,
    )(first, grad_fourier, legendre.reshape(128, 640))
    got = pltpu.with_memory_space_constraint(lax.all_to_all(send, ("yl", "x"), 0, 0), pltpu.VMEM)
    part = pl.pallas_call(
        mm_kernel,
        out_shape=pltpu.VMEM((32, 32, 128), F32),
        in_specs=[vm],
        out_specs=vm,
        scratch_shapes=[pltpu.VMEM((4, 32, 8, 128), F32)],
    )(got)
    part = lax.all_to_all(part.astype(F16), ("yh", "yl", "zh"), 0, 0)
    part = part.reshape(4, 2, 4, 32, 128).astype(F32)
    code, down = part[:, :, :, 30:31, :], jnp.float32(2.0**-8)
    for k in range(1, LEVELS):
        down = jnp.where(code == k, jnp.float32(2.0 ** -(8 + 18 * k)), down)
    part = pltpu.with_memory_space_constraint(jnp.sum(part * down, axis=(0, 2)), pltpu.VMEM)
    blocks = pl.pallas_call(
        blocks_kernel, out_shape=jax.ShapeDtypeStruct((6, 10, 128), F32), in_specs=[vm], out_specs=vm
    )(part)
    mine = lax.all_to_all(blocks, ("zl", "core"), 0, 0)
    input_grad, spec = pl.pallas_call(
        input_kernel,
        out_shape=(jax.ShapeDtypeStruct((5, 2, 2, 384), F32), pltpu.VMEM((6, 10, 128), F32)),
        in_specs=[vm, vm, vm],
        out_specs=(vm, vm),
        cost_estimate=pl.CostEstimate(flops=100000, bytes_accessed=200000, transcendentals=0),
    )(part, filter_weight, spectra)
    weight_grad = pl.pallas_call(
        weight_kernel,
        out_shape=jax.ShapeDtypeStruct((5, 2, 64), F32),
        in_specs=[vm, vm],
        out_specs=vm,
        scratch_shapes=[pltpu.VMEM((16, 128), F32)],
    )(*(pltpu.with_memory_space_constraint(v, pltpu.VMEM) for v in (mine, spec)))
    return input_grad, weight_grad


def solution(mesh):
    fine = Mesh(mesh.devices.reshape(4, 4, 4, 2, 3, 2), AXES)
    lat, ma = ("x", "zh", "yh", "yl"), ("zl", "core")
    in_specs = (P(ma, lat, None, None), P(ma, lat, None), P(lat, None, None, ma), P(lat, None, None))
    out_specs = (P(lat, ma, None, None), P(lat, None, ma))
    return jax.shard_map(body, mesh=fine, in_specs=in_specs, out_specs=out_specs, check_vma=False)
```

```python
import jax
import jax.numpy as jnp
from jax import lax
from jax.experimental import pallas as pl
from jax.experimental.pallas import tpu as pltpu
from jax.sharding import Mesh, PartitionSpec as P

BF, F16, F32 = jnp.bfloat16, jnp.float16, jnp.float32
AXES = ("x", "zh", "yh", "yl", "zl", "core")
LEVELS = 7


def pack_kernel(order_ref, grad_ref, leg_ref, out_ref):
    eye = jnp.where(
        lax.broadcasted_iota(jnp.int32, (128, 128), 0) == lax.broadcasted_iota(jnp.int32, (128, 128), 1), 1.0, 0.0
    ).astype(BF)
    order = order_ref[0] + jnp.where(lax.broadcasted_iota(jnp.int32, (128, 128), 1) >= 64, 1, 0)
    ahead = lax.broadcasted_iota(jnp.int32, (128, 128), 0) - order
    tiles = []
    for k in range(5):
        turned = lax.dot_general(
            eye, leg_ref[:, 128 * k:128 * (k + 1)], (((1,), (1,)), ((), ())), preferred_element_type=F32
        )
        tiles.append(jnp.where(ahead >= -128 * k, turned, 0.0))
    table = jnp.concatenate(tiles, axis=0)
    n = lax.broadcasted_iota(jnp.int32, (256, 256), 0)
    part = jnp.where(
        lax.broadcasted_iota(jnp.int32, (256, 256), 1) == (n % 128) * 2 + n // 128, 1.0, 0.0
    ).astype(BF)
    grad = jnp.dot(part, grad_ref[...].reshape(256, 384), preferred_element_type=F32).astype(BF)
    early = lax.broadcasted_iota(jnp.int32, (80, 128), 1) < 64
    for x in range(4):
        one, two = table[160 * x:160 * x + 80], table[160 * x + 80:160 * x + 160]
        halves = (
            jnp.where(early, one, pltpu.roll(two, 64, 1)),
            jnp.where(early, pltpu.roll(one, 64, 1), two),
        )
        for m in range(2):
            out_ref[2 * x + m, 0:80, :] = halves[m].astype(BF)
            for r in range(2):
                for j in range(3):
                    row = 80 + 64 * (3 * r + j)
                    out_ref[2 * x + m, row:row + 64, :] = grad[
                        128 * r + 64 * m:128 * r + 64 * m + 64, 128 * j:128 * (j + 1)
                    ]


def mm_kernel(in_ref, out_ref, acc_ref):
    n = lax.broadcasted_iota(jnp.int32, (160, 160), 0)
    src = (n % 4) * 40 + ((n % 32) // 4) * 5 + n // 32
    pick = jnp.where(lax.broadcasted_iota(jnp.int32, (160, 160), 1) == src, 1.0, 0.0).astype(BF)
    early = lax.broadcasted_iota(jnp.int32, (80, 128), 1) < 64
    low, high, rhs = [], [], []
    for s in range(0, 8, 2):
        one, two = in_ref[s, 0:80, :].astype(F32), in_ref[s + 1, 0:80, :].astype(F32)
        low.append(jnp.where(early, one, pltpu.roll(two, 64, 1)).astype(BF))
        high.append(jnp.where(early, pltpu.roll(one, 64, 1), two).astype(BF))
    for s in range(8):
        rhs.append(jnp.concatenate([in_ref[s, 80 + 64 * j:144 + 64 * j, :] for j in range(6)], axis=1))
    table = jnp.concatenate([jnp.concatenate(low, axis=1), jnp.concatenate(high, axis=1)], axis=0)
    table = jnp.dot(pick, table, preferred_element_type=F32).astype(BF)
    acc = jnp.dot(table, jnp.concatenate(rhs, axis=0), preferred_element_type=F32)
    top = jnp.max(jnp.abs(acc))
    up, code = jnp.float32(2.0**8), jnp.float32(0.0)
    for k in range(1, LEVELS):
        small = top < 2.0 ** (7 - 18 * k)
        up = jnp.where(small, jnp.float32(2.0 ** (8 + 18 * k)), up)
        code = jnp.where(small, jnp.float32(k), code)
    for j in range(6):
        part = (acc[:, 128 * j:128 * (j + 1)] * up).reshape(5, 4, 8, 128)
        for i in range(5):
            for d in range(4):
                acc_ref[d, i * 6 + j] = part[i, d]
    for d in range(4):
        acc_ref[d, 30:32] = jnp.full((2, 8, 128), code, F32)
        out_ref[8 * d:8 * (d + 1)] = jnp.swapaxes(acc_ref[d], 0, 1)


def blocks_kernel(in_ref, out_ref):
    early = lax.broadcasted_iota(jnp.int32, (5, 128), 1) < 64
    for m in range(2):
        for j in range(3):
            re, im = (in_ref[m, pl.ds(3 * r + j, 5, stride=6), :] for r in range(2))
            out_ref[2 * j, 5 * m:5 * m + 5] = jnp.where(early, re, pltpu.roll(im, 64, 1))
            out_ref[2 * j + 1, 5 * m:5 * m + 5] = jnp.where(early, pltpu.roll(re, 64, 1), im)


def final_kernel(in_ref, grad_ref, weight_ref, spec_ref, input_ref, out_ref):
    for j in range(3):
        wre, wim = (weight_ref[:, r, 128 * j:128 * (j + 1)] for r in range(2))
        for m in range(2):
            gre, gim = (in_ref[m, pl.ds(3 * r + j, 5, stride=6), :] for r in range(2))
            input_ref[:, m, 0, 128 * j:128 * (j + 1)] = wre * gre + wim * gim
            input_ref[:, m, 1, 128 * j:128 * (j + 1)] = wre * gim - wim * gre
    spec = jnp.concatenate([spec_ref[:, :, r, :].astype(F32) for r in range(2)], axis=2)
    total = jnp.zeros((5, 128), F32)
    early = lax.broadcasted_iota(jnp.int32, (5, 128), 1) < 64
    for m in range(12):
        grad, turned = grad_ref[m // 2, 5 * (m % 2):5 * (m % 2) + 5], spec[:, m, :]
        same, cross = turned * grad, turned * pltpu.roll(grad, 64, 1)
        total = total + jnp.where(
            early, same + pltpu.roll(same, 64, 1), pltpu.roll(cross, 64, 1) - cross
        )
    out_ref[:, 0, :] = total[:, 0:64]
    out_ref[:, 1, :] = total[:, 64:128]


def body(grad_fourier, legendre, spectra, filter_weight):
    first = ((lax.axis_index("zl") * 2 + lax.axis_index("core")) * 2).astype(jnp.int32).reshape(1)
    vm = pl.BlockSpec(memory_space=pltpu.VMEM)
    send = pl.pallas_call(
        pack_kernel,
        out_shape=pltpu.VMEM((8, 464, 128), BF),
        in_specs=[pl.BlockSpec(memory_space=pltpu.SMEM), vm, vm],
        out_specs=vm,
    )(first, grad_fourier, legendre.reshape(128, 640))
    got = pltpu.with_memory_space_constraint(lax.all_to_all(send, ("x", "yl"), 0, 0), pltpu.VMEM)
    part = pl.pallas_call(
        mm_kernel,
        out_shape=pltpu.VMEM((32, 32, 128), F32),
        in_specs=[vm],
        out_specs=vm,
        scratch_shapes=[pltpu.VMEM((4, 32, 8, 128), F32)],
    )(got)
    part = lax.all_to_all(part.astype(F16), ("yh", "yl", "zh"), 0, 0)
    part = part.reshape(4, 2, 4, 32, 128).astype(F32)
    code, down = part[:, :, :, 30:31, :], jnp.float32(2.0**-8)
    for k in range(1, LEVELS):
        down = jnp.where(code == k, jnp.float32(2.0 ** -(8 + 18 * k)), down)
    part = pltpu.with_memory_space_constraint(jnp.sum(part * down, axis=(0, 2)), pltpu.VMEM)
    blocks = pl.pallas_call(
        blocks_kernel, out_shape=pltpu.VMEM((6, 10, 128), F32), in_specs=[vm], out_specs=vm
    )(part)
    mine = pltpu.with_memory_space_constraint(lax.all_to_all(blocks, ("zl", "core"), 0, 0), pltpu.VMEM)
    input_grad, weight_grad = pl.pallas_call(
        final_kernel,
        out_shape=(jax.ShapeDtypeStruct((5, 2, 2, 384), F32), jax.ShapeDtypeStruct((5, 2, 64), F32)),
        in_specs=[vm, vm, vm, vm],
        out_specs=(vm, vm),
    )(part, mine, filter_weight, spectra)
    return input_grad, weight_grad


def solution(mesh):
    fine = Mesh(mesh.devices.reshape(4, 4, 4, 2, 3, 2), AXES)
    lat, ma = ("x", "zh", "yh", "yl"), ("zl", "core")
    in_specs = (P(ma, lat, None, None), P(ma, lat, None), P(lat, None, None, ma), P(lat, None, None))
    out_specs = (P(lat, ma, None, None), P(lat, None, ma))
    return jax.shard_map(body, mesh=fine, in_specs=in_specs, out_specs=out_specs, check_vma=False)
```

```python
import jax
import jax.numpy as jnp
from jax import lax
from jax.experimental import pallas as pl
from jax.experimental.pallas import tpu as pltpu
from jax.sharding import Mesh, PartitionSpec as P

BF, F16, F32 = jnp.bfloat16, jnp.float16, jnp.float32
AXES = ("x", "zh", "yh", "yl", "zl", "core")
LEVELS = 7


def pack_kernel(order_ref, grad_ref, leg_ref, out_ref):
    eye = jnp.where(
        lax.broadcasted_iota(jnp.int32, (128, 128), 0) == lax.broadcasted_iota(jnp.int32, (128, 128), 1), 1.0, 0.0
    ).astype(BF)
    order = order_ref[0] + jnp.where(lax.broadcasted_iota(jnp.int32, (128, 128), 1) >= 64, 1, 0)
    ahead = lax.broadcasted_iota(jnp.int32, (128, 128), 0) - order
    tiles = []
    for k in range(5):
        turned = lax.dot_general(
            eye, leg_ref[:, 128 * k:128 * (k + 1)], (((1,), (1,)), ((), ())), preferred_element_type=F32
        )
        tiles.append(jnp.where(ahead >= -128 * k, turned, 0.0))
    table = jnp.concatenate(tiles, axis=0)
    n = lax.broadcasted_iota(jnp.int32, (256, 256), 0)
    part = jnp.where(
        lax.broadcasted_iota(jnp.int32, (256, 256), 1) == (n % 128) * 2 + n // 128, 1.0, 0.0
    ).astype(BF)
    grad = jnp.dot(part, grad_ref[...].reshape(256, 384), preferred_element_type=F32).astype(BF)
    early = lax.broadcasted_iota(jnp.int32, (80, 128), 1) < 64
    for x in range(4):
        one, two = table[160 * x:160 * x + 80], table[160 * x + 80:160 * x + 160]
        halves = (
            jnp.where(early, one, pltpu.roll(two, 64, 1)),
            jnp.where(early, pltpu.roll(one, 64, 1), two),
        )
        for m in range(2):
            out_ref[2 * x + m, 0:80, :] = halves[m].astype(BF)
            for r in range(2):
                for j in range(3):
                    row = 80 + 64 * (3 * r + j)
                    out_ref[2 * x + m, row:row + 64, :] = grad[
                        128 * r + 64 * m:128 * r + 64 * m + 64, 128 * j:128 * (j + 1)
                    ]


def mm_kernel(in_ref, out_ref, acc_ref):
    n = lax.broadcasted_iota(jnp.int32, (160, 160), 0)
    src = (n % 4) * 40 + ((n % 32) // 4) * 5 + n // 32
    pick = jnp.where(lax.broadcasted_iota(jnp.int32, (160, 160), 1) == src, 1.0, 0.0).astype(BF)
    early = lax.broadcasted_iota(jnp.int32, (80, 128), 1) < 64
    low, high, rhs = [], [], []
    for s in range(0, 8, 2):
        one, two = in_ref[s, 0:80, :].astype(F32), in_ref[s + 1, 0:80, :].astype(F32)
        low.append(jnp.where(early, one, pltpu.roll(two, 64, 1)).astype(BF))
        high.append(jnp.where(early, pltpu.roll(one, 64, 1), two).astype(BF))
    for s in range(8):
        rhs.append(jnp.concatenate([in_ref[s, 80 + 64 * j:144 + 64 * j, :] for j in range(6)], axis=1))
    table = jnp.concatenate([jnp.concatenate(low, axis=1), jnp.concatenate(high, axis=1)], axis=0)
    table = jnp.dot(pick, table, preferred_element_type=F32).astype(BF)
    acc = jnp.dot(table, jnp.concatenate(rhs, axis=0), preferred_element_type=F32)
    top = jnp.max(jnp.abs(acc))
    up, code = jnp.float32(2.0**8), jnp.float32(0.0)
    for k in range(1, LEVELS):
        small = top < 2.0 ** (7 - 18 * k)
        up = jnp.where(small, jnp.float32(2.0 ** (8 + 18 * k)), up)
        code = jnp.where(small, jnp.float32(k), code)
    for j in range(6):
        part = (acc[:, 128 * j:128 * (j + 1)] * up).reshape(5, 4, 8, 128)
        for i in range(5):
            for d in range(4):
                acc_ref[d, i * 6 + j] = part[i, d]
    for d in range(4):
        acc_ref[d, 30:32] = jnp.full((2, 8, 128), code, F32)
        out_ref[8 * d:8 * (d + 1)] = jnp.swapaxes(acc_ref[d], 0, 1)


def blocks_kernel(in_ref, out_ref):
    early = lax.broadcasted_iota(jnp.int32, (5, 128), 1) < 64
    for m in range(2):
        for j in range(3):
            re, im = (in_ref[m, pl.ds(3 * r + j, 5, stride=6), :] for r in range(2))
            out_ref[2 * j, 5 * m:5 * m + 5] = jnp.where(early, re, pltpu.roll(im, 64, 1))
            out_ref[2 * j + 1, 5 * m:5 * m + 5] = jnp.where(early, pltpu.roll(re, 64, 1), im)


def final_kernel(in_ref, grad_ref, weight_ref, spec_ref, input_ref, out_ref):
    for j in range(3):
        wre, wim = (weight_ref[:, r, 128 * j:128 * (j + 1)] for r in range(2))
        for m in range(2):
            gre, gim = (in_ref[m, pl.ds(3 * r + j, 5, stride=6), :] for r in range(2))
            input_ref[:, m, 0, 128 * j:128 * (j + 1)] = wre * gre + wim * gim
            input_ref[:, m, 1, 128 * j:128 * (j + 1)] = wre * gim - wim * gre
    spec = jnp.concatenate([spec_ref[:, :, r, :].astype(F32) for r in range(2)], axis=2)
    total = jnp.zeros((5, 128), F32)
    early = lax.broadcasted_iota(jnp.int32, (5, 128), 1) < 64
    for m in range(12):
        grad, turned = grad_ref[m // 2, 5 * (m % 2):5 * (m % 2) + 5], spec[:, m, :]
        same, cross = turned * grad, turned * pltpu.roll(grad, 64, 1)
        total = total + jnp.where(
            early, same + pltpu.roll(same, 64, 1), pltpu.roll(cross, 64, 1) - cross
        )
    out_ref[:, 0, :] = total[:, 0:64]
    out_ref[:, 1, :] = total[:, 64:128]


def body(grad_fourier, legendre, spectra, filter_weight):
    first = ((lax.axis_index("zl") * 2 + lax.axis_index("core")) * 2).astype(jnp.int32).reshape(1)
    vm = pl.BlockSpec(memory_space=pltpu.VMEM)
    send = pl.pallas_call(
        pack_kernel,
        out_shape=pltpu.VMEM((8, 464, 128), BF),
        in_specs=[pl.BlockSpec(memory_space=pltpu.SMEM), vm, vm],
        out_specs=vm,
    )(first, grad_fourier, legendre.reshape(128, 640))
    got = pltpu.with_memory_space_constraint(lax.all_to_all(send, ("x", "yl"), 0, 0), pltpu.VMEM)
    part = pl.pallas_call(
        mm_kernel,
        out_shape=pltpu.VMEM((32, 32, 128), F32),
        in_specs=[vm],
        out_specs=vm,
        scratch_shapes=[pltpu.VMEM((4, 32, 8, 128), F32)],
    )(got)
    part = lax.all_to_all(part.astype(F16), ("yh", "yl", "zh"), 0, 0)
    part = part.reshape(4, 2, 4, 32, 128).astype(F32)
    code, down = part[:, :, :, 30:31, :], jnp.float32(2.0**-8)
    for k in range(1, LEVELS):
        down = jnp.where(code == k, jnp.float32(2.0 ** -(8 + 18 * k)), down)
    part = pltpu.with_memory_space_constraint(jnp.sum(part * down, axis=(0, 2)), pltpu.VMEM)
    blocks = pl.pallas_call(
        blocks_kernel, out_shape=pltpu.VMEM((6, 10, 128), F32), in_specs=[vm], out_specs=vm
    )(part)
    mine = pltpu.with_memory_space_constraint(lax.all_to_all(blocks, ("zl", "core"), 0, 0), pltpu.VMEM)
    input_grad, weight_grad = pl.pallas_call(
        final_kernel,
        out_shape=(jax.ShapeDtypeStruct((5, 2, 2, 384), F32), jax.ShapeDtypeStruct((5, 2, 64), F32)),
        in_specs=[vm, vm, vm, vm],
        out_specs=(vm, vm),
    )(part, mine, *(pltpu.with_memory_space_constraint(v, pltpu.VMEM) for v in (filter_weight, spectra)))
    return input_grad, weight_grad


def solution(mesh):
    fine = Mesh(mesh.devices.reshape(4, 4, 4, 2, 3, 2), AXES)
    lat, ma = ("x", "zh", "yh", "yl"), ("zl", "core")
    in_specs = (P(ma, lat, None, None), P(ma, lat, None), P(lat, None, None, ma), P(lat, None, None))
    out_specs = (P(lat, ma, None, None), P(lat, None, ma))
    return jax.shard_map(body, mesh=fine, in_specs=in_specs, out_specs=out_specs, check_vma=False)
```
